32 devices in a mesh: grp: 4 (over y, core), tp: 4 (over z), sec: 2 (over x).
Axes of the slice: x: 2, y: 2, z: 4, core: 2. Of those that a mesh axis runs over, the one named last changes fastest.
Arguments:
- layer_in: bfloat16 [2, 256, 4, 8192], P('sec', 'grp', None, 'tp'), may hold values from -6 to 6
- q_weight: bfloat16 [2, 8192, 8192], P('sec', 'grp', 'tp'), may hold values from -0.0625 to 0.0625
- kv_weight: bfloat16 [2, 8192, 2048], P('sec', 'grp', 'tp'), may hold values from -0.0625 to 0.0625
- o_weight: bfloat16 [2, 8192, 8192], P('sec', 'tp', 'grp'), may hold values from -0.5 to 0.5
- kv_cache: bfloat16 [2, 256, 4096, 256], P('sec', 'grp', 'tp'), may hold values from -600 to 600
- cache_lengths: int32 [256], P('grp'), may hold values from 1 to 512, as said below
- value_head: float32 [8192], P('tp'), may hold values from -0.0625 to 0.0625
Outputs:
- hidden_out: bfloat16 [2, 256, 4, 8192], P('sec', 'grp', None, 'tp')
- token_gap: float32 [256, 4], P('grp', 'sec')
The draws below stay inside these ranges and needn't reach their ends.
Inputs may be any that keep to these rules, and one draw needn't show every extreme that they name: `cache_lengths`: every rollout has at least one cached position; some rollout fills the whole cache and some holds a single position. Positions at or after a rollout's length hold arbitrary values.
All inputs are finite; a program needn't handle non-finite values.
Results may differ from the reference program's by a relative error of at most 0.018.
Values may be sent and summed in bfloat16 or wider, within the bound.
No kernel may reach another device: no remote copies, remote signals or barrier semaphores. Data moves between devices by JAX's collectives and lax.ppermute only.
A program may use at most 256 MiB of HBM per device.

```python
import jax
import jax.numpy as jnp
from jax import lax

D = 8192
H = 64
KVH = 8
HD = 128
R_DEV = 64
CACHE = 512
NSTEP = 4
R = 256
N_GRP = 4


def draw_cache_lengths(key, part):
    first_key, second_key, third_key = jax.random.split(jax.random.fold_in(key, 11), 3)
    factor_a = jax.random.randint(first_key, (R,), 1, 17)
    factor_b = jax.random.randint(second_key, (R,), 1, 17)
    lengths = 1 + factor_a * factor_b * (CACHE - 1) // 256
    chosen = jax.random.randint(third_key, (), 0, R)
    index = jnp.arange(R)
    lengths = jnp.where(index == chosen, CACHE, lengths)
    lengths = jnp.where(index == (chosen + 1) % R, 1, lengths)
    return lengths.astype(jnp.int32)


def draw_kv_cache(key, part):
    base_key = jax.random.fold_in(jax.random.fold_in(key, 23), 0)
    shape = (2, R, KVH, CACHE, 2, HD)
    values = jnp.clip(jax.random.normal(base_key, shape, jnp.float32), -4.0, 4.0)
    return values.reshape(2, R, KVH * CACHE, 2 * HD).astype(jnp.bfloat16)


def levels(key, shape, cuts, smallest, top_value):
    loudness = 1.0
    for dim, shards_of in cuts:
        heights = jax.random.uniform(jax.random.fold_in(jax.random.fold_in(key, 6), dim), (shards_of,), jnp.float32, smallest / len(cuts), top_value / len(cuts))
        loudness = loudness * jnp.repeat(jnp.exp(heights), shape[dim] // shards_of).reshape((-1,) + (1,) * (len(shape) - 1 - dim))
    return loudness


def noise(rng, dims, width, limit, cuts=(), held_as=jnp.bfloat16):
    drawn = width * jax.random.normal(rng, dims, jnp.float32)
    if cuts:
        drawn = drawn * levels(rng, dims, cuts, -0.22, 0.18)
    return jnp.clip(drawn, -limit, limit).astype(held_as)


def setup_inputs(seed: int = 0) -> dict:
    key_list = jax.random.split(jax.random.key(seed), 8)
    layer_in = noise(key_list[0], (2, R, NSTEP, D), 1.0, 6.0, ((0, 2), (1, 4), (3, 4)))
    q_weight = noise(key_list[1], (2, D, H * HD), D ** -0.5, 0.0625, ((0, 2), (1, 4), (2, 4)))
    kv_weight = noise(key_list[2], (2, D, 2 * KVH * HD), D ** -0.5, 0.0625, ((0, 2), (1, 4), (2, 4)))
    o_weight = noise(key_list[3], (2, H * HD, D), (H * HD // 64) ** -0.5, 0.5, ((0, 2), (1, 4), (2, 4)))
    kv_cache = draw_kv_cache(jax.random.fold_in(key_list[7], 71), 0)
    cache_lengths = draw_cache_lengths(jax.random.fold_in(key_list[7], 71), 0)
    value_head = noise(key_list[6], (D,), D ** -0.5, 0.0625, ((0, 4),), jnp.float32)
    return {"layer_in": layer_in, "q_weight": q_weight, "kv_weight": kv_weight, "o_weight": o_weight, "kv_cache": kv_cache, "cache_lengths": cache_lengths, "value_head": value_head}


def rounded(values):
    return lax.optimization_barrier(values.astype(jnp.bfloat16)).astype(jnp.float32)


def attend(block):
    query, new_key, new_value, cache, lengths = block
    rows = query.shape[0]
    cache_f = cache.astype(jnp.float32).reshape(rows, KVH, CACHE, 2, HD)
    cache_keys = cache_f[:, :, :, 0, :]
    cache_vals = cache_f[:, :, :, 1, :]
    score_scale = HD ** -0.5
    cache_scores = jnp.einsum('rskgd,rkpd->rskgp', query, cache_keys) * score_scale
    new_scores = jnp.einsum('rskgd,rtkd->rskgt', query, new_key) * score_scale
    visible = (jnp.arange(CACHE)[None, :] < lengths[:, None])[:, None, None, None, :]
    causal = (jnp.arange(NSTEP)[None, :] <= jnp.arange(NSTEP)[:, None])[None, :, None, None, :]
    row_peak = jnp.maximum(jnp.max(jnp.where(visible, cache_scores, -1e30), axis=-1),
                           jnp.max(jnp.where(causal, new_scores, -1e30), axis=-1))
    cache_w = jnp.where(visible, jnp.exp(cache_scores - row_peak[..., None]), 0.0)
    new_w = jnp.where(causal, jnp.exp(new_scores - row_peak[..., None]), 0.0)
    row_total = jnp.sum(cache_w, axis=-1) + jnp.sum(new_w, axis=-1)
    weighted = jnp.einsum('rskgp,rkpd->rskgd', rounded(cache_w), cache_vals)
    weighted = weighted + jnp.einsum('rskgt,rtkd->rskgd', rounded(new_w), new_value)
    return (weighted / row_total[..., None]).astype(jnp.bfloat16)


def section(layer_x, wq, wkv, wo, cache, lengths):
    flat = layer_x.reshape(R * NSTEP, D)
    query = rounded(jnp.dot(flat, wq, preferred_element_type=jnp.float32))
    query = query.reshape(N_GRP, R_DEV, NSTEP, KVH, H // KVH, HD)
    new_kv = rounded(jnp.dot(flat, wkv, preferred_element_type=jnp.float32))
    new_kv = new_kv.reshape(N_GRP, R_DEV, NSTEP, KVH, 2, HD)
    blocks = (query, new_kv[:, :, :, :, 0, :], new_kv[:, :, :, :, 1, :],
              cache.reshape(N_GRP, R_DEV, KVH * CACHE, 2 * HD), lengths.reshape(N_GRP, R_DEV))
    context = lax.map(attend, blocks).reshape(R * NSTEP, H * HD)
    result = jnp.dot(context, wo, preferred_element_type=jnp.float32).astype(jnp.bfloat16)
    return result.reshape(R, NSTEP, D)


def reference(layer_in, q_weight, kv_weight, o_weight, kv_cache, cache_lengths, value_head):
    policy = section(layer_in[0], q_weight[0], kv_weight[0], o_weight[0], kv_cache[0], cache_lengths)
    refer = section(layer_in[1], q_weight[1], kv_weight[1], o_weight[1], kv_cache[1], cache_lengths)
    hidden_out = jnp.stack([policy, refer])
    diff = policy.astype(jnp.float32) - refer.astype(jnp.float32)
    token_gap = jnp.sum(diff * value_head, axis=-1)
    return hidden_out, token_gap
```

```python
import functools
import jax
import jax.numpy as jnp
from jax import lax
from jax.experimental import pallas as pl
from jax.experimental.pallas import tpu as pltpu
from jax.sharding import PartitionSpec as P

KVH = 8
HD = 128
CACHE = 512
PIECES = 2


def swap(value, axis, mask):
    if mask == 0:
        return value
    pairs = [(source, source ^ mask) for source in range(lax.axis_size(axis))]
    return lax.ppermute(value, axis, pairs)


def attend_kernel(lens_ref, lead_ref, q_ref, new_ref, cache_ref, *outs, steps, first, partial):
    blocks, heads, rows, _ = q_ref.shape
    span = cache_ref.shape[2] // heads
    base = pl.program_id(0) * blocks + first
    lead = lead_ref[0]
    nt = (((1,), (1,)), ((), ()))
    nn = (((1,), (0,)), ((), ()))
    scale = HD ** (-0.5)
    spot = lax.broadcasted_iota(jnp.int32, (rows, span), 1)
    step_of_row = lax.broadcasted_iota(jnp.int32, (rows, steps), 0) % steps
    step_of_col = lax.broadcasted_iota(jnp.int32, (rows, steps), 1)
    causal = (step_of_col <= step_of_row) & (lead > 0)
    for b in range(blocks):
        visible = spot < lens_ref[base + b]
        for j in range(heads):
            q = q_ref[b, j]
            keys = cache_ref[0, b, j * span : (j + 1) * span, :HD]
            vals = cache_ref[0, b, j * span : (j + 1) * span, HD:]
            new_keys = new_ref[b, j, :, :HD]
            new_vals = new_ref[b, j, :, HD:]
            score = lax.dot_general(q, keys, nt, preferred_element_type=jnp.float32) * scale
            fresh = lax.dot_general(q, new_keys, nt, preferred_element_type=jnp.float32) * scale
            score = jnp.where(visible, score, -1e30)
            fresh = jnp.where(causal, fresh, -1e30)
            peak = jnp.maximum(
                jnp.max(score, axis=1, keepdims=True), jnp.max(fresh, axis=1, keepdims=True)
            )
            weight = jnp.where(visible, jnp.exp(score - peak), 0.0)
            fresh_w = jnp.where(causal, jnp.exp(fresh - peak), 0.0)
            total = jnp.sum(weight, axis=1, keepdims=True) + jnp.sum(
                fresh_w, axis=1, keepdims=True
            )
            acc = lax.dot_general(
                weight.astype(jnp.bfloat16), vals, nn, preferred_element_type=jnp.float32
            )
            acc = acc + lax.dot_general(
                fresh_w.astype(jnp.bfloat16), new_vals, nn, preferred_element_type=jnp.float32
            )
            if partial:
                outs[0][b, j] = acc
                lane = lax.broadcasted_iota(jnp.int32, (rows, HD), 1)
                outs[1][b, j] = jnp.where(lane == 0, peak, total)
            else:
                outs[0][b, j] = (acc / total).astype(jnp.bfloat16)


def attend(lens, lead, query, fresh, cache, first, partial):
    count, heads, rows, _ = query.shape
    steps = fresh.shape[2]
    blocks = 4
    while count % blocks:
        blocks //= 2
    skip = first // blocks
    held = (blocks, heads, rows, HD)
    at = lambda i, *_: (i, 0, 0, 0)
    out_spec = pl.BlockSpec(held, at)
    shape = (count, heads, rows, HD)
    if partial:
        out_specs = [out_spec, out_spec]
        out_shape = [jax.ShapeDtypeStruct(shape, jnp.float32)] * 2
    else:
        out_specs = out_spec
        out_shape = jax.ShapeDtypeStruct(shape, jnp.bfloat16)
    return pl.pallas_call(
        functools.partial(attend_kernel, steps=steps, first=first, partial=partial),
        grid_spec=pltpu.PrefetchScalarGridSpec(
            num_scalar_prefetch=2,
            grid=(count // blocks,),
            in_specs=[
                pl.BlockSpec(held, at),
                pl.BlockSpec((blocks, heads, steps, 2 * HD), at),
                pl.BlockSpec(
                    (1, blocks, cache.shape[2], 2 * HD), lambda i, *_: (0, i + skip, 0, 0)
                ),
            ],
            out_specs=out_specs,
        ),
        out_shape=out_shape,
        name="attend",
    )(lens, lead, query, fresh, cache)


def local(layer_in, q_weight, kv_weight, o_weight, kv_cache, cache_lengths, value_head):
    tp = lax.axis_size("tp")
    tp_place = lax.axis_index("tp")
    grp = lax.axis_size("grp")
    grp_place = lax.axis_index("grp")
    sec = lax.axis_size("sec")
    sec_place = lax.axis_index("sec")
    rollouts, steps, width = layer_in.shape[1:]
    per_row = tp // grp
    query_cols = q_weight.shape[2]
    pair_size = max(tp // KVH, 1)
    is_even = tp_place % 2 == 0
    rows_dev = kv_cache.shape[2]
    start_pos = tp_place * rows_dev % CACHE
    lens = cache_lengths - start_pos
    lead = (tp_place % pair_size == 0).astype(jnp.int32).reshape(1)
    weight_q = q_weight[0].reshape(per_row, width, query_cols)
    weight_kv = kv_weight[0].reshape(per_row, width, -1)
    weight_o = o_weight[0].reshape(o_weight.shape[1], per_row, width)
    pieces = PIECES
    part = rollouts // pieces
    tokens = part * steps
    order = list(range(grp))
    far_bits = [b for b in reversed(range(grp.bit_length() - 1))]

    head_all = lax.all_gather(value_head, "tp", axis=0, tiled=True).reshape(grp, per_row, width)
    head_mine = lax.dynamic_index_in_dim(head_all, grp_place, 0, keepdims=False)

    def to_rows(piece):
        block = layer_in[0, piece * part : (piece + 1) * part].reshape(tokens, width)
        full = lax.all_gather(block, "tp", axis=0)
        full = full.reshape(grp, per_row, tokens, width)
        got = {}
        for mask in sorted(order, reverse=True):
            mine = lax.dynamic_index_in_dim(full, grp_place ^ mask, 0, keepdims=False)
            got[mask] = swap(mine, "grp", mask)
        return got

    def project(got):
        stack = jnp.concatenate([got[mask] for mask in order], axis=1)
        q = jnp.einsum("mtf,mfc->tc", stack, weight_q, preferred_element_type=jnp.float32)
        kv = jnp.einsum("mtf,mfc->tc", stack, weight_kv, preferred_element_type=jnp.float32)
        both = jnp.concatenate([q.astype(jnp.bfloat16), kv.astype(jnp.bfloat16)], axis=1)
        sums = {mask: both[i * tokens : (i + 1) * tokens] for i, mask in enumerate(order)}
        bit = 1
        while bit < grp:
            keep = [mask for mask in sums if not mask & bit]
            send = jnp.concatenate([sums[mask | bit] for mask in keep], axis=0)
            came = swap(send, "grp", bit)
            sums = {
                mask: (
                    sums[mask].astype(jnp.float32)
                    + came[i * tokens : (i + 1) * tokens].astype(jnp.float32)
                ).astype(jnp.bfloat16)
                for i, mask in enumerate(keep)
            }
            bit *= 2
        return sums[0]

    def look(piece, both):
        query = both[:, :query_cols]
        pair = both[:, query_cols:]
        if pair_size > 1:
            other_q, other_p = swap(query, "tp", 1), swap(pair, "tp", 1)
            query = jnp.concatenate(
                [jnp.where(is_even, query, other_q), jnp.where(is_even, other_q, query)], axis=1
            )
            pair = jnp.concatenate(
                [jnp.where(is_even, pair, other_p), jnp.where(is_even, other_p, pair)], axis=1
            )
        heads = pair.shape[1] // (2 * HD)
        groups = query.shape[1] // (heads * HD)
        query = query.reshape(part, steps, heads, groups, HD).transpose(0, 2, 3, 1, 4)
        query = query.reshape(part, heads, groups * steps, HD)
        fresh = pair.reshape(part, steps, heads, 2 * HD).transpose(0, 2, 1, 3)
        found = attend(lens, lead, query, fresh, kv_cache, piece * part, pair_size > 1)
        if pair_size > 1:
            acc, stat = found
            half = groups * steps // 2

            def halves(x):
                low, high = x[:, :, :half], x[:, :, half:]
                return jnp.where(is_even, low, high), jnp.where(is_even, high, low)

            keep_acc, send_acc = halves(acc)
            keep_stat, send_stat = halves(stat[..., :2])
            came_acc = swap(send_acc.astype(jnp.bfloat16), "tp", 1)
            came_stat = swap(send_stat, "tp", 1)
            peak = jnp.maximum(keep_stat[..., :1], came_stat[..., :1])
            own = jnp.exp(keep_stat[..., :1] - peak)
            far = jnp.exp(came_stat[..., :1] - peak)
            total = keep_stat[..., 1:] * own + came_stat[..., 1:] * far
            found = ((keep_acc * own + came_acc * far) / total).astype(jnp.bfloat16)
            groups = groups // 2
        found = found.reshape(part, heads, groups, steps, HD).transpose(0, 3, 1, 2, 4)
        return found.reshape(tokens, heads * groups * HD)

    def spread(context):
        held = {0: context}
        for bit in far_bits:
            held.update({mask | 2**bit: swap(held[mask], "grp", 2**bit) for mask in list(held)})
        return held

    def finish(held):
        stack = jnp.concatenate([held[mask] for mask in order], axis=0)
        terms = jnp.einsum("tr,rmf->mtf", stack, weight_o, preferred_element_type=jnp.float32)
        gap = jnp.sum(terms * head_mine[:, None, :], axis=(0, 2))
        terms = terms.astype(jnp.bfloat16)
        slots = jnp.zeros((grp, per_row, tokens, width), jnp.bfloat16)
        for mask in sorted(order, reverse=True):
            got = swap(terms[:, mask * tokens : (mask + 1) * tokens], "grp", mask)
            slots = lax.dynamic_update_index_in_dim(slots, got, grp_place ^ mask, 0)
        result = lax.psum_scatter(
            slots.reshape(tp, tokens, width), "tp", scatter_dimension=0, tiled=False
        )
        return result, gap

    results, gaps = [], []
    for piece in range(pieces):
        got = to_rows(piece)
        both = project(got)
        context = look(piece, both)
        result, gap = finish(spread(context))
        results.append(result.reshape(part, steps, width))
        gaps.append(gap.reshape(grp, part, steps))
    hidden_out = jnp.concatenate(results, axis=0)[None]
    gap_all = jnp.concatenate(gaps, axis=1)
    gap_all = gap_all * jnp.where(sec_place == 0, 1.0, -1.0)
    ordered = jnp.stack([
        lax.dynamic_index_in_dim(gap_all, grp_place ^ mask, 0, keepdims=False) for mask in order
    ])
    whole = lax.psum(ordered, ("sec", "grp", "tp"))
    own = lax.dynamic_index_in_dim(whole, grp_place, 0, keepdims=False)
    share = steps // sec
    own_gap = lax.dynamic_slice_in_dim(own, sec_place * share, share, 1)
    return hidden_out, own_gap


def solution(mesh):
    placed = (
        P("sec", "grp", None, "tp"),
        P("sec", "grp", "tp"),
        P("sec", "grp", "tp"),
        P("sec", "tp", "grp"),
        P("sec", "grp", "tp", None),
        P("grp"),
        P("tp"),
    )
    return jax.shard_map(
        local,
        mesh=mesh,
        in_specs=placed,
        out_specs=(P("sec", "grp", None, "tp"), P("grp", "sec")),
        check_vma=False,
    )
```
